1024 devices in a mesh: expert: 32 (over x, y), cuts: 2 (over core), dp: 16 (over z).
Axes of the slice: x: 4, y: 8, z: 16, core: 2. Of those that a mesh axis runs over, the one named last changes fastest.
Arguments:
- activations: bfloat16 [65536, 2048], P(('expert', 'dp')), may hold values from -6 to 6
- out_grad: bfloat16 [65536, 2048], P(('expert', 'dp')), may hold values from -6 to 6
- expert_ids: int32 [65536, 1], P(('expert', 'dp')), may hold values from 0 to 31; in each aligned block of 128 rows (0 to 127, 128 to 255, ...) at most 5 rows name the same one
- gate_up_weight: bfloat16 [32, 2048, 2, 768], P('expert', None, None, 'cuts'), may hold values from -0.125 to 0.125
- down_weight: bfloat16 [32, 2048, 768], P('expert', None, 'cuts'), may hold values from -0.21875 to 0.21875
- master_weight: float32 [32, 2048, 3, 768], P('expert', 'dp', None, 'cuts'), may hold values from -6 to 6
- first_moment: bfloat16 [32, 2048, 3, 768], P('expert', 'dp', None, 'cuts'), may hold values from -6 to 6
- second_moment: bfloat16 [32, 2048, 3, 768], P('expert', 'dp', None, 'cuts'), may hold values from 0.5 to 8
- new_owner: int32 [32, 32], replicated, may hold values from 0 to 31, each once within a row
Outputs:
- input_grad: bfloat16 [65536, 2048], P(('expert', 'dp'), 'cuts')
- moved_master: float32 [32, 32, 64, 3, 768], P('expert', None, 'dp', None, 'cuts')
- moved_first: bfloat16 [32, 32, 64, 3, 768], P('expert', None, 'dp', None, 'cuts')
- moved_second: bfloat16 [32, 32, 64, 3, 768], P('expert', None, 'dp', None, 'cuts')
The draws below stay inside these ranges and needn't reach their ends.
Inputs may be any that keep to these rules, and one draw needn't show every extreme that they name: `expert_ids`: within the 128 rows of one device no expert is named by more than 5 rows, and in every draw some device names some expert exactly 5 times. `new_owner`: each row names every owner index exactly once.
All inputs are finite; a program needn't handle non-finite values.
Results may differ from the reference program's by a relative error of at most 0.019.
Values may be sent and summed in bfloat16 or wider, within the bound.
A program may use at most 64 MiB of HBM per device.

```python
import math
import jax
import jax.numpy as jnp
import numpy as np
from jax import lax

D = 2048
FF = 768
ROWS_DEV = 128
EXPERTS = 32
CAP = 5
ROWS = 65536
N_EXPERT = 32
N_CUTS = 2
N_DP = 16


def levels(key, dims, shards, least, top_value):
    def one(dim, shards_of):
        heights = jax.random.uniform(jax.random.fold_in(jax.random.fold_in(key, 6), dim), (shards_of,), jnp.float32, least / len(shards), top_value / len(shards))
        return jnp.repeat(jnp.exp(heights), dims[dim] // shards_of).reshape((-1,) + (1,) * (len(dims) - dim - 1))

    loudness = one(*shards[0])
    for cut in shards[1:]:
        loudness = loudness * one(*cut)
    return loudness


def deal_out(own_key, own, number, rows, count, top, most, slope):
    ranking = jax.random.permutation(own_key, count)
    heavy_load, common = portions_of(count, rows * top, most, slope, True), portions_of(count, rows * top, most, slope, False)
    places = jnp.arange(count)

    def named(lengths, offset_by):
        used = int((lengths > 0).sum())
        fixed = max(1, used // 4)
        passed = fixed + (places - fixed + offset_by * (used - fixed)) % max(1, count - fixed)
        return jnp.zeros((count,), jnp.int32).at[ranking[jnp.where(places < fixed, places, passed)]].set(jnp.asarray(lengths, jnp.int32))

    lengths = jnp.where(number % 4 == 0, named(heavy_load, number // 4), named(common, number - number // 4 - 1))
    mixed = jax.random.permutation(jax.random.fold_in(own, 3), count)
    giver, taker = mixed[0:count // 2 * 2:2], mixed[1:count // 2 * 2:2]
    slack = jnp.minimum(lengths[giver] - 1, most - lengths[taker]) // 2
    slack = jnp.where((giver == ranking[0]) | (taker == ranking[0]) | (lengths[taker] == 0), 0, jnp.maximum(slack, 0))
    passed = jax.random.randint(jax.random.fold_in(own, 4), (count // 2,), 0, 1 << 20) % (slack + 1)
    lengths = lengths.at[giver].add(-passed).at[taker].add(passed)
    labels = jnp.searchsorted(jnp.cumsum(lengths), jnp.arange(rows * top), side="right").astype(jnp.int32)
    table = labels.reshape(top, rows).T
    table = table[jax.random.permutation(jax.random.fold_in(own, 1), rows)]
    offset_by = jax.random.randint(jax.random.fold_in(own, 2), (rows, 1), 0, top)
    return jnp.take_along_axis(table, (jnp.arange(top)[None, :] + offset_by) % top, axis=1)


def portions_of(amount, total, reach, slope, full):
    weights = [(1 << 20) // math.isqrt(grade ** slope) + 1 for grade in range(1, amount + 1)]
    largest = reach if full else min(reach, max(-(-total // amount), total * weights[0] // sum(weights)))
    least = 1 if total - largest >= amount - 1 else 0
    holding, surplus = [largest] + [least] * (amount - 1), total - largest - least * (amount - 1)
    while surplus > 0:
        candidates = [i for i in range(1, amount) if holding[i] < largest] or [i for i in range(1, amount) if holding[i] < reach]
        whole, left = sum([weights[i] for i in candidates]), surplus
        for i in candidates:
            more = min(reach - holding[i], max(1, left * weights[i] // whole), surplus)
            holding[i] = holding[i] + more
            surplus = surplus - more
    return np.array(holding)


def noise(key, shape, width, most, cuts=(), held_as=jnp.bfloat16):
    entries = jax.random.normal(key, shape, jnp.float32) * width
    if len(cuts) > 0:
        entries = levels(key, shape, cuts, -0.22, 0.18) * entries
    return jnp.clip(entries, min=-most, max=most).astype(held_as)


def setup_inputs(seed: int = 0) -> dict:
    arg_keys = jax.random.split(jax.random.key(seed), 10)
    activations = noise(arg_keys[0], (ROWS, D), 1.0, 6.0, ((0, 512),))
    out_grad = noise(arg_keys[1], (ROWS, D), 1.0, 6.0, ((0, 512),))
    expert_ids_keys = jax.random.split(jax.random.fold_in(arg_keys[2], 1), ROWS // ROWS_DEV)
    expert_ids_turns = jax.random.permutation(jax.random.fold_in(arg_keys[2], 3), ROWS // ROWS_DEV)
    expert_ids = jax.vmap(lambda own, number: deal_out(jax.random.fold_in(arg_keys[2], 2), own, number, ROWS_DEV, EXPERTS, 1, CAP, 2))(expert_ids_keys, expert_ids_turns).reshape((ROWS, 1))
    gate_up_weight = noise(arg_keys[3], (EXPERTS, D, 2, FF), D ** -0.5, 0.125, ((0, 32), (3, 2)))
    down_weight = noise(arg_keys[4], (EXPERTS, D, FF), FF ** -0.5, 0.21875, ((0, 32), (2, 2)))
    master_weight = noise(arg_keys[5], (EXPERTS, D, 3, FF), 1.0, 6.0, ((0, 32), (1, 16), (3, 2)), jnp.float32)
    first_moment = noise(arg_keys[6], (EXPERTS, D, 3, FF), 1.0, 6.0, ((0, 32), (1, 16), (3, 2)))
    second_moment = jnp.clip(jnp.exp(math.log(8.0) - 2.7725887 * jax.random.uniform(arg_keys[7], (EXPERTS, D, 3, FF), jnp.float32) ** levels(arg_keys[7], (EXPERTS, D, 3, FF), ((0, 32), (1, 16), (3, 2)), -0.2, 0.2)), 0.5, 8.0).astype(jnp.bfloat16)
    new_owner = jax.vmap(lambda own: jax.random.permutation(own, N_EXPERT))(jax.random.split(arg_keys[8], EXPERTS)).reshape((EXPERTS, N_EXPERT)).astype(jnp.int32)
    return {"activations": activations, "out_grad": out_grad, "expert_ids": expert_ids, "gate_up_weight": gate_up_weight, "down_weight": down_weight, "master_weight": master_weight, "first_moment": first_moment, "second_moment": second_moment, "new_owner": new_owner}


beta_first = 0.9
beta_second = 0.95
learn_rate = 0.01
decay_rate = 0.1
epsilon = 1e-08

def route(values, positions):
    experts = positions.shape[0]
    data_count = positions.shape[1]
    source = jnp.arange(experts, dtype=jnp.int32)[:, None, None]
    replica = jnp.arange(data_count, dtype=jnp.int32)[None, :, None]
    filled = jnp.zeros((experts, data_count, experts * CAP, D), jnp.bfloat16)
    filled = filled.at[source, replica, positions].set(values)
    filled = filled.reshape(experts, data_count, experts, CAP, D).transpose(2, 1, 0, 3, 4)
    return filled.reshape(experts, data_count, experts * CAP, D)

def expert_pass(inputs):
    routed_in, routed_grad, gate_up, down = inputs
    features = routed_in.astype(jnp.float32)
    cotangents = routed_grad.astype(jnp.float32)
    gate_matrix = gate_up[:, 0, :].astype(jnp.float32)
    lift_matrix = gate_up[:, 1, :].astype(jnp.float32)
    down_matrix = down.astype(jnp.float32)
    gate_value = jnp.einsum('prd,df->prf', features, gate_matrix)
    lift_value = jnp.einsum('prd,df->prf', features, lift_matrix)
    sigmoid_gate = jax.nn.sigmoid(gate_value)
    silu_gate = gate_value * sigmoid_gate
    hidden = (silu_gate * lift_value).astype(jnp.bfloat16)
    hidden_grad = jnp.einsum('prd,df->prf', cotangents, down_matrix)
    lift_grad = (hidden_grad * silu_gate).astype(jnp.bfloat16)
    gate_grad = (hidden_grad * lift_value * sigmoid_gate * (1.0 + gate_value * (1.0 - sigmoid_gate))).astype(jnp.bfloat16)
    block_width = FF // N_CUTS
    total_grad = jnp.zeros(features.shape, jnp.float32)
    for block_index in range(N_CUTS):
        lower = block_index * block_width
        upper = lower + block_width
        block_grad = jnp.einsum('prf,df->prd', gate_grad[:, :, lower:upper].astype(jnp.float32), gate_matrix[:, lower:upper])
        block_grad = block_grad + jnp.einsum('prf,df->prd', lift_grad[:, :, lower:upper].astype(jnp.float32), lift_matrix[:, lower:upper])
        rounded = lax.optimization_barrier(block_grad.astype(jnp.bfloat16))
        total_grad = total_grad + rounded.astype(jnp.float32)
    gate_part = jnp.einsum('prd,prf->pdf', features, gate_grad.astype(jnp.float32))
    lift_part = jnp.einsum('prd,prf->pdf', features, lift_grad.astype(jnp.float32))
    down_part = jnp.einsum('prd,prf->pdf', cotangents, hidden.astype(jnp.float32))
    stacked = lax.optimization_barrier(jnp.stack([gate_part, lift_part, down_part], axis=2).astype(jnp.bfloat16))
    gradient = lax.optimization_barrier(jnp.sum(stacked.astype(jnp.float32), axis=0)) / N_DP
    return (total_grad.astype(jnp.bfloat16), gradient)

def migrate(tensor, inverse):
    slice_rows = D // (N_EXPERT * N_DP)
    pieces = tensor.reshape(N_EXPERT, N_DP, N_EXPERT, slice_rows, 3, FF)
    picked = jnp.take_along_axis(pieces, inverse[:, None, :, None, None, None], axis=2)
    return picked.transpose(2, 0, 1, 3, 4, 5).reshape(N_EXPERT, N_EXPERT, N_DP * slice_rows, 3, FF)

def reference(activations, out_grad, expert_ids, gate_up_weight, down_weight, master_weight, first_moment, second_moment, new_owner):
    row_expert = expert_ids.reshape(N_EXPERT, N_DP, ROWS_DEV)
    onehot = (row_expert[..., None] == jnp.arange(N_EXPERT, dtype=jnp.int32)).astype(jnp.int32)
    within = lax.optimization_barrier(jnp.sum(jnp.cumsum(onehot, axis=2) * onehot, axis=3)) - 1
    positions = (row_expert * CAP + within).astype(jnp.int32)
    routed_in = route(activations.reshape(N_EXPERT, N_DP, ROWS_DEV, D), positions)
    routed_grad = route(out_grad.reshape(N_EXPERT, N_DP, ROWS_DEV, D), positions)
    slot_grad, gradient = lax.map(expert_pass, (routed_in, routed_grad, gate_up_weight, down_weight))
    slot_grad = slot_grad.reshape(N_EXPERT, N_DP, N_EXPERT, CAP, D)
    source = jnp.arange(N_EXPERT, dtype=jnp.int32)[:, None, None]
    replica = jnp.arange(N_DP, dtype=jnp.int32)[None, :, None]
    input_grad = slot_grad[row_expert, replica, source, within].reshape(ROWS, D)
    first_new = beta_first * first_moment.astype(jnp.float32) + (1.0 - beta_first) * gradient
    second_new = beta_second * second_moment.astype(jnp.float32) + (1.0 - beta_second) * gradient * gradient
    master_new = master_weight - learn_rate * (first_new / (jnp.sqrt(second_new) + epsilon) + decay_rate * master_weight)
    inverse = jnp.argsort(new_owner, axis=1).astype(jnp.int32)
    moved_master = migrate(master_new, inverse)
    moved_first = migrate(first_new.astype(jnp.bfloat16), inverse)
    moved_second = migrate(second_new.astype(jnp.bfloat16), inverse)
    return (input_grad, moved_master, moved_first, moved_second)
```

```python
import functools

import jax
import jax.numpy as jnp
from jax import lax
from jax.experimental import pallas as pl
from jax.experimental.pallas import tpu as pltpu
from jax.sharding import PartitionSpec as P

beta_first = 0.9
beta_second = 0.95
learn_rate = 0.01
decay_rate = 0.1
epsilon = 1e-08

MESH = pl.DeviceIdType.MESH
LANES = 128
SLOT = 8
F32 = jnp.float32
BF16 = jnp.bfloat16


def one_hot(cond):
    return jnp.where(cond, 1.0, 0.0).astype(BF16)


def dot(a, b):
    return jnp.dot(a, b, preferred_element_type=F32)


def iota(shape, axis):
    return lax.broadcasted_iota(jnp.int32, shape, axis)


def ranks(ids_ref):
    n = ids_ref.shape[1]
    lane = jnp.broadcast_to(ids_ref[...].astype(F32), (n, n))
    sub = lane.T
    same = jnp.where(lane == sub, 1.0, 0.0)
    i, j = iota((n, n), 0), iota((n, n), 1)
    within_lane = jnp.sum(jnp.where(i < j, same, 0.0), axis=0, keepdims=True)
    within_sub = jnp.sum(jnp.where(j < i, same, 0.0), axis=1, keepdims=True)
    return lane[0:1].astype(jnp.int32), within_lane.astype(jnp.int32), sub, within_sub


def dispatch_kernel(
    n_e, ids_ref, act_ref, grad_ref, out_ref, send, ssem, rsem, fssem, frsem, lsem
):
    me, core = lax.axis_index("expert"), lax.axis_index("cuts")
    rows, width = act_ref.shape
    half = width // 2
    total = n_e * SLOT
    sibling = {"cuts": 1 - core}

    barrier = pltpu.get_barrier_semaphore()

    @pl.loop(1, n_e)
    def _(d):
        pl.semaphore_signal(
            barrier, inc=1, device_id={"expert": (me + d) % n_e}, device_id_type=MESH
        )

    pl.semaphore_signal(barrier, inc=1, device_id=sibling, device_id_type=MESH)

    ids, within, _, _ = ranks(ids_ref)
    row = iota((total, rows), 0)
    code_in = ids * SLOT + within
    code_grad = jnp.where(within < 3, ids * SLOT + 5 + within, -1)
    pick = jnp.concatenate([one_hot(row == code_in), one_hot(row == code_grad)], axis=1)
    columns = pl.ds(pl.multiple_of(core * half, half), half)
    both = jnp.concatenate([act_ref[:, columns], grad_ref[:, columns]], axis=0)
    send[:, :half] = dot(pick, both).astype(BF16)
    code_rest = jnp.where(within >= 3, ids * SLOT + within - 3, -1000)
    pick_rest = jnp.concatenate([one_hot(row == code_rest + 2 * l) for l in range(4)], axis=1)
    for u in range(2):
        tiles = [
            both[rows:, (4 * u + l) * LANES : (4 * u + l + 1) * LANES] for l in range(4)
        ]
        send[:, half + u * LANES : half + (u + 1) * LANES] = dot(
            pick_rest, jnp.concatenate(tiles, axis=0)
        ).astype(BF16)

    pl.semaphore_wait(barrier, n_e)

    def block(k):
        return pl.ds(pl.multiple_of(k * SLOT, SLOT), SLOT)

    def out_copy(d):
        return pltpu.make_async_remote_copy(
            src_ref=send.at[block((me + d) % n_e)],
            dst_ref=out_ref.at[core, block(me)],
            send_sem=ssem.at[d],
            recv_sem=rsem.at[d],
            device_id={"expert": (me + d) % n_e},
            device_id_type=MESH,
        )

    def forward(d):
        source = block((me + n_e - d) % n_e)
        return pltpu.make_async_remote_copy(
            src_ref=out_ref.at[core, source],
            dst_ref=out_ref.at[core, source],
            send_sem=fssem.at[d],
            recv_sem=frsem.at[d],
            device_id=sibling,
            device_id_type=MESH,
        )

    def forwarded(d):
        source = block((me + n_e - d) % n_e)
        return pltpu.make_async_remote_copy(
            src_ref=out_ref.at[1 - core, source],
            dst_ref=out_ref.at[1 - core, source],
            send_sem=fssem.at[d],
            recv_sem=frsem.at[d],
            device_id=sibling,
            device_id_type=MESH,
        )

    @pl.loop(1, n_e)
    def _(d):
        out_copy(d).start()

    own = pltpu.make_async_copy(send.at[block(me)], out_ref.at[core, block(me)], lsem)
    own.start()
    own.wait()
    forward(0).start()

    @pl.loop(1, n_e)
    def _(d):
        out_copy(d).wait_recv()
        forward(d).start()

    @pl.loop(0, n_e)
    def _(d):
        forwarded(d).wait_recv()
        forward(d).wait_send()

    @pl.loop(1, n_e)
    def _(d):
        out_copy(d).wait_send()


def expert_kernel(slots_ref, gate_up_ref, down_ref, part_ref, msg_ref, grads, picks, mids, back):
    total, half = slots_ref.shape[1], gate_up_ref.shape[1] // 2
    row = iota((total, total), 0)
    col = iota((total, total), 1)
    place = row % SLOT

    for l in range(4):
        picks[l, :, :total] = one_hot((place < 3) & (col == row + 5))
        picks[l, :, total:] = one_hot(
            ((place == 3) | (place == 4)) & (col == row - 3 + 2 * l)
        )
    for h in range(2):
        for t in range(half // LANES):
            u, l = t // 4, t % 4
            source = jnp.concatenate(
                [
                    slots_ref[h, :, t * LANES : (t + 1) * LANES],
                    slots_ref[h, :, half + u * LANES : half + (u + 1) * LANES],
                ],
                axis=0,
            )
            grads[:, h * half + t * LANES : h * half + (t + 1) * LANES] = dot(
                picks[l], source
            ).astype(BF16)

    first, second = slots_ref[0, :, :half], slots_ref[1, :, :half]
    gate = dot(first, gate_up_ref[0, :half]) + dot(second, gate_up_ref[0, half:])
    lift = dot(first, gate_up_ref[1, :half]) + dot(second, gate_up_ref[1, half:])
    hidden_grad = dot(grads[...], down_ref[...])
    sigmoid_gate = jax.nn.sigmoid(gate)
    silu_gate = gate * sigmoid_gate
    mids[0] = (hidden_grad * lift * sigmoid_gate * (1.0 + gate * (1.0 - sigmoid_gate))).astype(
        BF16
    )
    mids[1] = (hidden_grad * silu_gate).astype(BF16)
    mids[2] = (silu_gate * lift).astype(BF16)

    tile = 256
    over_rows = (((0,), (0,)), ((), ()))
    over_units = (((1,), (1,)), ((), ()))
    for h in range(2):

        @pl.loop(0, half // tile)
        def _(i, h=h):
            at = pl.ds(pl.multiple_of(i * tile, tile), tile)
            wide = pl.ds(pl.multiple_of(h * half + i * tile, tile), tile)
            ins = slots_ref[h, :, at]
            outs = grads[:, wide]
            for g in range(3):
                part_ref[g, wide, :] = lax.dot_general(
                    ins if g < 2 else outs, mids[g], over_rows, preferred_element_type=F32
                ).astype(BF16)
            back[:, wide] = (
                lax.dot_general(
                    mids[0], gate_up_ref[0, wide, :], over_units, preferred_element_type=F32
                )
                + lax.dot_general(
                    mids[1], gate_up_ref[1, wide, :], over_units, preferred_element_type=F32
                )
            ).astype(BF16)

    for m in range(5):
        shift = jnp.concatenate(
            [one_hot((place == 5 + t) & (col == row - 5 - t + m)) for t in range(3)], axis=1
        )
        for h in range(2):
            rest = jnp.concatenate(
                [back[:, h * half + (5 + t) * LANES : h * half + (6 + t) * LANES] for t in range(3)],
                axis=0,
            )
            base = back[:, h * half + m * LANES : h * half + (m + 1) * LANES]
            msg_ref[h, :, m * LANES : (m + 1) * LANES] = (
                base.astype(F32) + dot(shift, rest)
            ).astype(BF16)


def adam_update(master, first_old, second_old, gradient):
    first_new = beta_first * first_old + (1.0 - beta_first) * gradient
    second_new = beta_second * second_old + (1.0 - beta_second) * gradient * gradient
    master_new = master - learn_rate * (
        first_new / (jnp.sqrt(second_new) + epsilon) + decay_rate * master
    )
    return (master_new, first_new, second_new)


def update_kernel(
    n_e,
    n_p,
    part_ref,
    msg_ref,
    ids_ref,
    owner_ref,
    master_ref,
    first_ref,
    second_ref,
    ig_ref,
    moved_ref,
    ring,
    other,
    csend,
    crecv,
    msend,
    ring_s,
    ring_r,
    xsem,
    cs_sem,
    cr_sem,
    ms_sem,
    mr_sem,
    lsem,
):
    me, core, dp = lax.axis_index("expert"), lax.axis_index("cuts"), lax.axis_index("dp")
    shard = master_ref.shape[1]
    hop = shard // 2
    rows = ids_ref.shape[1]
    total = n_e * SLOT
    piece = shard // n_e
    sibling = {"cuts": 1 - core}
    ahead = ({"dp": (dp + 1) % n_p}, {"dp": (dp + n_p - 1) % n_p})

    barrier = pltpu.get_barrier_semaphore()

    @pl.loop(1, n_e)
    def _(d):
        pl.semaphore_signal(
            barrier, inc=1, device_id={"expert": (me + d) % n_e}, device_id_type=MESH
        )

    pl.semaphore_signal(barrier, inc=1, device_id=sibling, device_id_type=MESH)
    for to in ahead:
        pl.semaphore_signal(barrier, inc=1, device_id=to, device_id_type=MESH)
    pl.semaphore_wait(barrier, n_e + 2)

    def own(q, way):
        return pl.ds(pl.multiple_of(q * shard + way * hop, hop), hop)

    def shard_of(t, way):
        return (dp + n_p - 1 - t) % n_p if way == 0 else (dp + 1 + t) % n_p

    def ring_copy(t, g, way, src):
        return pltpu.make_async_remote_copy(
            src_ref=src,
            dst_ref=ring.at[t, g, way],
            send_sem=ring_s.at[t, g, way],
            recv_sem=ring_r.at[t, g, way],
            device_id=ahead[way],
            device_id_type=MESH,
        )

    streams = [(g, way) for g in range(3) for way in range(2)]
    for g, way in streams:
        ring_copy(0, g, way, part_ref.at[g, own(shard_of(0, way), way)]).start()

    swap = pltpu.make_async_remote_copy(
        src_ref=msg_ref.at[1 - core],
        dst_ref=other,
        send_sem=xsem.at[0],
        recv_sem=xsem.at[1],
        device_id=sibling,
        device_id_type=MESH,
    )
    swap.start()
    swap.wait_recv()
    csend[...] = (msg_ref[core].astype(F32) + other[...].astype(F32)).astype(BF16)

    def block(k):
        return pl.ds(pl.multiple_of(k * SLOT, SLOT), SLOT)

    def combine_copy(d):
        return pltpu.make_async_remote_copy(
            src_ref=csend.at[block((me + d) % n_e)],
            dst_ref=crecv.at[block(me)],
            send_sem=cs_sem.at[d],
            recv_sem=cr_sem.at[d],
            device_id={"expert": (me + d) % n_e},
            device_id_type=MESH,
        )

    @pl.loop(1, n_e)
    def _(d):
        combine_copy(d).start()

    keep = pltpu.make_async_copy(csend.at[block(me)], crecv.at[block(me)], lsem.at[0])
    keep.start()

    @pl.loop(1, n_p - 1)
    def _(t):
        for g, way in streams:
            held = ring.at[t - 1, g, way]
            ring_copy(t - 1, g, way, held).wait_recv()
            mine = part_ref[g, own(shard_of(t, way), way), :]
            held[...] = (held[...].astype(F32) + mine.astype(F32)).astype(BF16)
            ring_copy(t, g, way, held).start()

    owners = jnp.where(
        iota((n_e, n_e), 0) == me, owner_ref[...].astype(F32), 0.0
    ).astype(BF16)
    spread = one_hot(iota((n_e, shard), 1) // piece == iota((n_e, shard), 0))
    owner_of = jnp.sum(dot(owners, spread), axis=0, keepdims=True).astype(jnp.int32)
    code = owner_of * SLOT + iota((1, shard), 1) % piece
    arrange = one_hot(iota((total, shard), 0) == code)

    def move_copy(g, d):
        return pltpu.make_async_remote_copy(
            src_ref=msend.at[g, (me + d) % n_e],
            dst_ref=moved_ref.at[me, :, g],
            send_sem=ms_sem.at[g, d],
            recv_sem=mr_sem.at[g, d],
            device_id={"expert": (me + d) % n_e},
            device_id_type=MESH,
        )

    def move_keep(g):
        return pltpu.make_async_copy(
            msend.at[g, me], moved_ref.at[me, :, g], lsem.at[1 + g]
        )

    last = n_p - 2
    for g in range(3):
        sums = []
        for way in range(2):
            held = ring.at[last, g, way]
            ring_copy(last, g, way, held).wait_recv()
            sums.append(held[...].astype(F32) + part_ref[g, own(dp, way), :].astype(F32))
        gradient = jnp.concatenate(sums, axis=0) * (1.0 / n_p)
        new = adam_update(
            master_ref[g], first_ref[g].astype(F32), second_ref[g].astype(F32), gradient
        )
        for k in range(3):
            placed = dot(arrange, new[k].astype(BF16))
            placed = placed.reshape(n_e, SLOT, placed.shape[1])
            msend[g, :, k] = placed[:, :piece].astype(BF16)

        @pl.loop(1, n_e)
        def _(d, g=g):
            move_copy(g, d).start()

        move_keep(g).start()

    keep.wait()

    @pl.loop(1, n_e)
    def _(d):
        combine_copy(d).wait_recv()

    _, _, expert, within = ranks(ids_ref)
    expert = jnp.broadcast_to(expert[:, 0:1], (rows, total)).astype(jnp.int32)
    within = jnp.broadcast_to(within, (rows, total)).astype(jnp.int32)
    col = iota((rows, total), 1)
    ig_ref[:, : 5 * LANES] = dot(
        one_hot(col == expert * SLOT + within), crecv[...]
    ).astype(BF16)
    stacked = jnp.concatenate(
        [crecv[:, m * LANES : (m + 1) * LANES] for m in range(5)], axis=0
    )
    for t in range(3):
        pick = jnp.concatenate(
            [one_hot((col == expert * SLOT + 5 + t) & (within == m)) for m in range(5)], axis=1
        )
        ig_ref[:, (5 + t) * LANES : (6 + t) * LANES] = dot(pick, stacked).astype(BF16)

    swap.wait_send()

    @pl.loop(0, n_p - 1)
    def _(t):
        for g, way in streams:
            ring_copy(t, g, way, ring.at[t, g, way]).wait_send()

    @pl.loop(1, n_e)
    def _(d):
        combine_copy(d).wait_send()

    for g in range(3):
        move_keep(g).wait()

        @pl.loop(1, n_e)
        def _(d, g=g):
            move_copy(g, d).wait_recv()
            move_copy(g, d).wait_send()


VMEM = pl.BlockSpec(memory_space=pltpu.VMEM)


def local(
    activations,
    out_grad,
    expert_ids,
    gate_up_weight,
    down_weight,
    master_weight,
    first_moment,
    second_moment,
    new_owner,
):
    n_e = lax.axis_size("expert")
    n_p = lax.axis_size("dp")
    rows, width = activations.shape
    units = down_weight.shape[2]
    half = width // 2
    total = n_e * SLOT
    shard = width // n_p
    piece = shard // n_e
    ids = expert_ids.reshape(1, rows)
    dma = pltpu.SemaphoreType.DMA

    slots = pl.pallas_call(
        functools.partial(dispatch_kernel, n_e),
        name="dispatch",
        out_shape=jax.ShapeDtypeStruct((2, total, half + 2 * LANES), BF16),
        in_specs=[VMEM] * 3,
        out_specs=VMEM,
        scratch_shapes=[
            pltpu.VMEM((total, half + 2 * LANES), BF16),
            dma((n_e,)),
            dma((n_e,)),
            dma((n_e,)),
            dma((n_e,)),
            dma,
        ],
        compiler_params=pltpu.CompilerParams(collective_id=0, has_side_effects=True),
    )(ids, activations, out_grad)

    gate_up = jnp.moveaxis(gate_up_weight[0], 1, 0)
    part, msg = pl.pallas_call(
        expert_kernel,
        name="expert",
        out_shape=(
            jax.ShapeDtypeStruct((3, width, units), BF16),
            jax.ShapeDtypeStruct((2, total, 5 * LANES), BF16),
        ),
        in_specs=[VMEM] * 3,
        out_specs=(VMEM, VMEM),
        scratch_shapes=[
            pltpu.VMEM((total, width), BF16),
            pltpu.VMEM((4, total, 2 * total), BF16),
            pltpu.VMEM((3, total, units), BF16),
            pltpu.VMEM((total, width), BF16),
        ],
    )(slots, gate_up, down_weight[0])

    input_grad, moved = pl.pallas_call(
        functools.partial(update_kernel, n_e, n_p),
        name="update",
        out_shape=(
            jax.ShapeDtypeStruct((rows, half), BF16),
            jax.ShapeDtypeStruct((n_e, 3, 3, piece, units), BF16),
        ),
        in_specs=[VMEM] * 7,
        out_specs=(VMEM, VMEM),
        scratch_shapes=[
            pltpu.VMEM((n_p - 1, 3, 2, shard // 2, units), BF16),
            pltpu.VMEM((total, 5 * LANES), BF16),
            pltpu.VMEM((total, 5 * LANES), BF16),
            pltpu.VMEM((total, 5 * LANES), BF16),
            pltpu.VMEM((3, n_e, 3, piece, units), BF16),
            dma((n_p - 1, 3, 2)),
            dma((n_p - 1, 3, 2)),
            dma((2,)),
            dma((n_e,)),
            dma((n_e,)),
            dma((3, n_e)),
            dma((3, n_e)),
            dma((4,)),
        ],
        compiler_params=pltpu.CompilerParams(collective_id=1, has_side_effects=True),
    )(
        part,
        msg,
        ids,
        new_owner,
        jnp.moveaxis(master_weight[0], 1, 0),
        jnp.moveaxis(first_moment[0], 1, 0),
        jnp.moveaxis(second_moment[0], 1, 0),
    )
    moved = jnp.moveaxis(moved, 2, 3)
    return (
        input_grad,
        moved[:, 0].astype(F32)[None],
        moved[:, 1][None],
        moved[:, 2][None],
    )


def solution(mesh):
    in_specs = (
        P(("expert", "dp"), None),
        P(("expert", "dp"), None),
        P(("expert", "dp"), None),
        P("expert", None, None, "cuts"),
        P("expert", None, "cuts"),
        P("expert", "dp", None, "cuts"),
        P("expert", "dp", None, "cuts"),
        P("expert", "dp", None, "cuts"),
        P(),
    )
    out_specs = (
        P(("expert", "dp"), "cuts"),
        P("expert", None, "dp", None, "cuts"),
        P("expert", None, "dp", None, "cuts"),
        P("expert", None, "dp", None, "cuts"),
    )
    return jax.shard_map(local, mesh=mesh, in_specs=in_specs, out_specs=out_specs, check_vma=False)
```

```python
import functools

import jax
import jax.numpy as jnp
from jax import lax
from jax.experimental import pallas as pl
from jax.experimental.pallas import tpu as pltpu
from jax.sharding import PartitionSpec as P

beta_first = 0.9
beta_second = 0.95
learn_rate = 0.01
decay_rate = 0.1
epsilon = 1e-08

MESH = pl.DeviceIdType.MESH
LANES = 128
SLOT = 8
F32 = jnp.float32
BF16 = jnp.bfloat16


def one_hot(cond):
    return jnp.where(cond, 1.0, 0.0).astype(BF16)


def dot(a, b):
    return jnp.dot(a, b, preferred_element_type=F32)


def iota(shape, axis):
    return lax.broadcasted_iota(jnp.int32, shape, axis)


def ranks(ids_ref):
    n = ids_ref.shape[1]
    lane = jnp.broadcast_to(ids_ref[...].astype(F32), (n, n))
    sub = lane.T
    same = jnp.where(lane == sub, 1.0, 0.0)
    i, j = iota((n, n), 0), iota((n, n), 1)
    within_lane = jnp.sum(jnp.where(i < j, same, 0.0), axis=0, keepdims=True)
    within_sub = jnp.sum(jnp.where(j < i, same, 0.0), axis=1, keepdims=True)
    return lane[0:1].astype(jnp.int32), within_lane.astype(jnp.int32), sub, within_sub


def adam_update(master, first_old, second_old, gradient):
    first_new = beta_first * first_old + (1.0 - beta_first) * gradient
    second_new = beta_second * second_old + (1.0 - beta_second) * gradient * gradient
    master_new = master - learn_rate * (
        first_new / (jnp.sqrt(second_new) + epsilon) + decay_rate * master
    )
    return (master_new, first_new, second_new)


STAGGER = 2


def step_kernel(
    n_e,
    n_p,
    ids_ref,
    owner_ref,
    act_any,
    grad_any,
    gate_up_any,
    down_any,
    master_any,
    first_any,
    second_any,
    ig_ref,
    moved_ref,
    act,
    grad,
    raw,
    gate_up,
    down,
    master,
    first,
    second,
    send,
    slots,
    grads,
    picks,
    mids,
    back,
    msg,
    parts,
    begin,
    ring,
    other,
    csend,
    crecv,
    place_ref,
    msend,
    load_sem,
    keep_sem,
    ssem,
    rsem,
    fssem,
    frsem,
    ring_s,
    ring_r,
    xsem,
    cs_sem,
    cr_sem,
    ms_sem,
    mr_sem,
):
    me, core, dp = lax.axis_index("expert"), lax.axis_index("cuts"), lax.axis_index("dp")
    rows, half = act.shape
    width = 2 * half
    total = n_e * SLOT
    shard = master.shape[1]
    hop = shard // 2
    piece = shard // n_e
    per_half = half // shard
    sibling = {"cuts": 1 - core}
    ahead = ({"dp": (dp + 1) % n_p}, {"dp": (dp + n_p - 1) % n_p})

    def peer(d):
        return (me + d) % n_e

    def block(k):
        return pl.ds(pl.multiple_of(k * SLOT, SLOT), SLOT)

    columns = pl.ds(pl.multiple_of(core * half, half), half)
    loads = [
        pltpu.make_async_copy(src, dst, load_sem.at[i])
        for i, (src, dst) in enumerate(
            (
                (act_any.at[:, columns], act),
                (grad_any.at[:, columns], grad),
                (gate_up_any, raw),
                (down_any, down),
                (master_any, master),
                (first_any, first),
                (second_any, second),
            )
        )
    ]
    for load in loads:
        load.start()

    barrier = pltpu.get_barrier_semaphore()

    @pl.loop(1, n_e)
    def _(d):
        pl.semaphore_signal(
            barrier, inc=1, device_id={"expert": peer(d)}, device_id_type=MESH
        )

    for to in (sibling, *ahead):
        pl.semaphore_signal(barrier, inc=1, device_id=to, device_id_type=MESH)

    ids, within, _, _ = ranks(ids_ref)
    row = iota((total, rows), 0)
    code_in = ids * SLOT + within
    code_grad = jnp.where(within < 3, ids * SLOT + 5 + within, -1)
    pick = jnp.concatenate([one_hot(row == code_in), one_hot(row == code_grad)], axis=1)
    code_rest = jnp.where(within >= 3, ids * SLOT + within - 3, -1000)
    pick_rest = jnp.concatenate([one_hot(row == code_rest + 2 * l) for l in range(4)], axis=1)
    loads[0].wait()
    loads[1].wait()
    send[:, :half] = dot(pick, jnp.concatenate([act[...], grad[...]], axis=0)).astype(BF16)
    for u in range(2):
        tiles = [grad[:, (4 * u + l) * LANES : (4 * u + l + 1) * LANES] for l in range(4)]
        send[:, half + u * LANES : half + (u + 1) * LANES] = dot(
            pick_rest, jnp.concatenate(tiles, axis=0)
        ).astype(BF16)

    pl.semaphore_wait(barrier, n_e + 2)

    def out_copy(d):
        return pltpu.make_async_remote_copy(
            src_ref=send.at[block(peer(d))],
            dst_ref=slots.at[core, block(me)],
            send_sem=ssem.at[d],
            recv_sem=rsem.at[d],
            device_id={"expert": peer(d)},
            device_id_type=MESH,
        )

    def forward(d, from_core):
        at = slots.at[from_core, block((me + n_e - d) % n_e)]
        return pltpu.make_async_remote_copy(
            src_ref=at,
            dst_ref=at,
            send_sem=fssem.at[d],
            recv_sem=frsem.at[d],
            device_id=sibling,
            device_id_type=MESH,
        )

    @pl.loop(1, n_e)
    def _(d):
        out_copy(d).start()

    own = pltpu.make_async_copy(send.at[block(me)], slots.at[core, block(me)], keep_sem.at[0])
    own.start()
    own.wait()
    forward(0, core).start()

    loads[2].wait()
    lines = 256

    @pl.loop(0, width // lines)
    def _(i):
        at = pl.ds(pl.multiple_of(i * lines, lines), lines)
        gate_up[:, at, :] = jnp.swapaxes(raw[at], 0, 1)

    row2 = iota((total, total), 0)
    col2 = iota((total, total), 1)
    place = row2 % SLOT
    for l in range(4):
        picks[l, :, :total] = one_hot((place < 3) & (col2 == row2 + 5))
        picks[l, :, total:] = one_hot(
            ((place == 3) | (place == 4)) & (col2 == row2 - 3 + 2 * l)
        )
    owners = jnp.where(
        iota((n_e, n_e), 0) == me, owner_ref[...].astype(F32), 0.0
    ).astype(BF16)
    spread = one_hot(iota((n_e, shard), 1) // piece == iota((n_e, shard), 0))
    owner_of = jnp.sum(dot(owners, spread), axis=0, keepdims=True).astype(jnp.int32)
    code = owner_of * SLOT + iota((1, shard), 1) % piece
    place_ref[...] = one_hot(iota((total, shard), 0) == code)
    for load in loads[3:]:
        load.wait()

    @pl.loop(1, n_e)
    def _(d):
        out_copy(d).wait_recv()
        forward(d, core).start()

    @pl.loop(0, n_e)
    def _(d):
        forward(d, 1 - core).wait_recv()

    for h in range(2):
        for t in range(half // LANES):
            u, l = t // 4, t % 4
            source = jnp.concatenate(
                [
                    slots[h, :, t * LANES : (t + 1) * LANES],
                    slots[h, :, half + u * LANES : half + (u + 1) * LANES],
                ],
                axis=0,
            )
            grads[:, h * half + t * LANES : h * half + (t + 1) * LANES] = dot(
                picks[l], source
            ).astype(BF16)
    low, high = slots[0, :, :half], slots[1, :, :half]
    gate = dot(low, gate_up[0, :half]) + dot(high, gate_up[0, half:])
    lift = dot(low, gate_up[1, :half]) + dot(high, gate_up[1, half:])
    hidden_grad = dot(grads[...], down[...])
    sigmoid_gate = jax.nn.sigmoid(gate)
    silu_gate = gate * sigmoid_gate
    mids[0] = (hidden_grad * lift * sigmoid_gate * (1.0 + gate * (1.0 - sigmoid_gate))).astype(
        BF16
    )
    mids[1] = (hidden_grad * silu_gate).astype(BF16)
    mids[2] = (silu_gate * lift).astype(BF16)

    def shard_of(t, way):
        return (dp + n_p - 1 - t) % n_p if way == 0 else (dp + 1 + t) % n_p

    def share(g, q, way):
        if g < 2:
            at = pl.ds(pl.multiple_of((q % per_half) * shard, shard), shard)
            lhs = slots[q // per_half, :, at]
        else:
            lhs = grads[:, pl.ds(pl.multiple_of(q * shard, shard), shard)]
        return dot(lhs.T[way * hop : (way + 1) * hop], mids[g])

    def ring_copy(t, g, way, src):
        return pltpu.make_async_remote_copy(
            src_ref=src,
            dst_ref=ring.at[t, g, way],
            send_sem=ring_s.at[t, g, way],
            recv_sem=ring_r.at[t, g, way],
            device_id=ahead[way],
            device_id_type=MESH,
        )

    def ring_start(g):
        for way in range(2):
            begin[g, way] = share(g, shard_of(0, way), way).astype(BF16)
            ring_copy(0, g, way, begin.at[g, way]).start()

    def ring_step(step, active, extra):
        for g in active:
            for way in range(2):
                parts[g, way] = share(g, shard_of(step - g * STAGGER, way), way)
        if extra is not None:
            extra(step)
        for g in active:
            for way in range(2):
                t = step - g * STAGGER
                held = ring.at[t - 1, g, way]
                ring_copy(t - 1, g, way, held).wait_recv()
                held[...] = (held[...].astype(F32) + parts[g, way]).astype(BF16)
                ring_copy(t, g, way, held).start()

    tile = 256
    over_units = (((1,), (1,)), ((), ()))

    def rows_back(step):
        for j in range(2):
            wide = pl.ds(pl.multiple_of((step - 1) * (2 * tile) + j * tile, tile), tile)
            back[:, wide] = (
                lax.dot_general(
                    mids[0], gate_up[0, wide, :], over_units, preferred_element_type=F32
                )
                + lax.dot_general(
                    mids[1], gate_up[1, wide, :], over_units, preferred_element_type=F32
                )
            ).astype(BF16)

    back_steps = width // (2 * tile)

    def pack_back(step):
        m = step - 1 - back_steps
        shift = jnp.concatenate(
            [one_hot((place == 5 + t) & (col2 == row2 - 5 - t + m)) for t in range(3)], axis=1
        )
        for h in range(2):
            rest = jnp.concatenate(
                [back[:, h * half + (5 + t) * LANES : h * half + (6 + t) * LANES] for t in range(3)],
                axis=0,
            )
            base = back[:, pl.ds(pl.multiple_of(h * half + m * LANES, LANES), LANES)]
            msg[h, :, pl.ds(pl.multiple_of(m * LANES, LANES), LANES)] = (
                base.astype(F32) + dot(shift, rest)
            ).astype(BF16)

    swap = pltpu.make_async_remote_copy(
        src_ref=msg.at[1 - core],
        dst_ref=other,
        send_sem=xsem.at[0],
        recv_sem=xsem.at[1],
        device_id=sibling,
        device_id_type=MESH,
    )

    def combine_copy(d):
        return pltpu.make_async_remote_copy(
            src_ref=csend.at[block(peer(d))],
            dst_ref=crecv.at[block(me)],
            send_sem=cs_sem.at[d],
            recv_sem=cr_sem.at[d],
            device_id={"expert": peer(d)},
            device_id_type=MESH,
        )

    keep = pltpu.make_async_copy(csend.at[block(me)], crecv.at[block(me)], keep_sem.at[1])

    def combine(step):
        swap.wait_recv()
        csend[...] = (msg[core].astype(F32) + other[...].astype(F32)).astype(BF16)

        @pl.loop(1, n_e)
        def _(d):
            combine_copy(d).start()

        keep.start()

    def move_copy(g, d):
        return pltpu.make_async_remote_copy(
            src_ref=msend.at[g, peer(d)],
            dst_ref=moved_ref.at[me, :, g],
            send_sem=ms_sem.at[g, d],
            recv_sem=mr_sem.at[g, d],
            device_id={"expert": peer(d)},
            device_id_type=MESH,
        )

    def move_keep(g):
        return pltpu.make_async_copy(
            msend.at[g, me], moved_ref.at[me, :, g], keep_sem.at[2 + g]
        )

    last = n_p - 2

    def finish(g):
        sums = []
        for way in range(2):
            held = ring.at[last, g, way]
            ring_copy(last, g, way, held).wait_recv()
            sums.append(held[...].astype(F32) + parts[g, way])
        gradient = jnp.concatenate(sums, axis=0) * (1.0 / n_p)
        new = adam_update(
            master[g], first[g].astype(F32), second[g].astype(F32), gradient
        )
        for k in range(3):
            placed = dot(place_ref[...], new[k].astype(BF16))
            placed = placed.reshape(n_e, SLOT, placed.shape[1])
            msend[g, :, k] = placed[:, :piece].astype(BF16)

        @pl.loop(1, n_e)
        def _(d):
            move_copy(g, d).start()

        move_keep(g).start()

    def plan(step):
        starts = tuple(g for g in range(3) if step == g * STAGGER)
        active = tuple(g for g in range(3) if 1 <= step - g * STAGGER <= last)
        ends = tuple(g for g in range(3) if step - g * STAGGER == last + 1)
        if 1 <= step <= back_steps:
            extra = rows_back
        elif back_steps < step <= back_steps + 5:
            extra = pack_back
        else:
            extra = None
        return starts, active, ends, extra

    swap_at = back_steps + 6
    step, stop = 0, last + 2 + 2 * STAGGER
    while step < stop:
        starts, active, ends, extra = plan(step)
        if step == swap_at:
            swap.start()
        if step == swap_at + 1:
            extra = combine
        special = starts or ends or step in (swap_at, swap_at + 1)
        until = step + 1
        while not special and until < stop and until not in (swap_at, swap_at + 1):
            if plan(until) != (starts, active, ends, extra):
                break
            until += 1
        if until - step > 1:

            @pl.loop(step, until)
            def _(s, active=active, extra=extra):
                ring_step(s, active, extra)

        else:
            ring_step(step, active, extra)
        for g in starts:
            ring_start(g)
        for g in ends:
            for way in range(2):
                parts[g, way] = share(g, dp, way)
            finish(g)
        step = until

    keep.wait()

    @pl.loop(1, n_e)
    def _(d):
        combine_copy(d).wait_recv()

    _, _, expert, within = ranks(ids_ref)
    expert = jnp.broadcast_to(expert[:, 0:1], (rows, total)).astype(jnp.int32)
    within = jnp.broadcast_to(within, (rows, total)).astype(jnp.int32)
    col = iota((rows, total), 1)
    ig_ref[:, : 5 * LANES] = dot(
        one_hot(col == expert * SLOT + within), crecv[...]
    ).astype(BF16)
    stacked = jnp.concatenate(
        [crecv[:, m * LANES : (m + 1) * LANES] for m in range(5)], axis=0
    )
    for t in range(3):
        pick = jnp.concatenate(
            [one_hot((col == expert * SLOT + 5 + t) & (within == m)) for m in range(5)], axis=1
        )
        ig_ref[:, (5 + t) * LANES : (6 + t) * LANES] = dot(pick, stacked).astype(BF16)

    swap.wait_send()

    @pl.loop(1, n_e)
    def _(d):
        out_copy(d).wait_send()
        combine_copy(d).wait_send()

    @pl.loop(0, n_e)
    def _(d):
        forward(d, core).wait_send()

    @pl.loop(0, n_p - 1)
    def _(t):
        for g in range(3):
            for way in range(2):
                ring_copy(t, g, way, ring.at[t, g, way]).wait_send()

    for g in range(3):
        move_keep(g).wait()

        @pl.loop(1, n_e)
        def _(d, g=g):
            move_copy(g, d).wait_recv()
            move_copy(g, d).wait_send()


VMEM = pl.BlockSpec(memory_space=pltpu.VMEM)
ANY = pl.BlockSpec(memory_space=pl.ANY)


def local(
    activations,
    out_grad,
    expert_ids,
    gate_up_weight,
    down_weight,
    master_weight,
    first_moment,
    second_moment,
    new_owner,
):
    n_e = lax.axis_size("expert")
    n_p = lax.axis_size("dp")
    rows, width = activations.shape
    units = down_weight.shape[2]
    half = width // 2
    total = n_e * SLOT
    shard = width // n_p
    piece = shard // n_e
    line = half + 2 * LANES
    dma = pltpu.SemaphoreType.DMA

    def vmem(*shape, dtype=BF16):
        return pltpu.VMEM(shape, dtype)

    input_grad, moved = pl.pallas_call(
        functools.partial(step_kernel, n_e, n_p),
        name="step",
        out_shape=(
            jax.ShapeDtypeStruct((rows, half), BF16),
            jax.ShapeDtypeStruct((n_e, 3, 3, piece, units), BF16),
        ),
        in_specs=[VMEM] * 2 + [ANY] * 7,
        out_specs=(VMEM, VMEM),
        scratch_shapes=[
            vmem(rows, half),
            vmem(rows, half),
            vmem(width, 2, units),
            vmem(2, width, units),
            vmem(width, units),
            vmem(3, shard, units, dtype=F32),
            vmem(3, shard, units),
            vmem(3, shard, units),
            vmem(total, line),
            vmem(2, total, line),
            vmem(total, width),
            vmem(4, total, 2 * total),
            vmem(3, total, units),
            vmem(total, width),
            vmem(2, total, 5 * LANES),
            vmem(3, 2, shard // 2, units, dtype=F32),
            vmem(3, 2, shard // 2, units),
            vmem(n_p - 1, 3, 2, shard // 2, units),
            vmem(total, 5 * LANES),
            vmem(total, 5 * LANES),
            vmem(total, 5 * LANES),
            vmem(total, shard),
            vmem(3, n_e, 3, piece, units),
            dma((7,)),
            dma((5,)),
            dma((n_e,)),
            dma((n_e,)),
            dma((n_e,)),
            dma((n_e,)),
            dma((n_p - 1, 3, 2)),
            dma((n_p - 1, 3, 2)),
            dma((2,)),
            dma((n_e,)),
            dma((n_e,)),
            dma((3, n_e)),
            dma((3, n_e)),
        ],
        compiler_params=pltpu.CompilerParams(collective_id=0, has_side_effects=True),
    )(
        expert_ids.reshape(1, rows),
        new_owner,
        activations,
        out_grad,
        gate_up_weight[0],
        down_weight[0],
        jnp.moveaxis(master_weight[0], 1, 0),
        jnp.moveaxis(first_moment[0], 1, 0),
        jnp.moveaxis(second_moment[0], 1, 0),
    )
    moved = jnp.moveaxis(moved, 2, 3)
    return (
        input_grad,
        moved[:, 0].astype(F32)[None],
        moved[:, 1][None],
        moved[:, 2][None],
    )


def solution(mesh):
    in_specs = (
        P(("expert", "dp"), None),
        P(("expert", "dp"), None),
        P(("expert", "dp"), None),
        P("expert", None, None, "cuts"),
        P("expert", None, "cuts"),
        P("expert", "dp", None, "cuts"),
        P("expert", "dp", None, "cuts"),
        P("expert", "dp", None, "cuts"),
        P(),
    )
    out_specs = (
        P(("expert", "dp"), "cuts"),
        P("expert", None, "dp", None, "cuts"),
        P("expert", None, "dp", None, "cuts"),
        P("expert", None, "dp", None, "cuts"),
    )
    return jax.shard_map(local, mesh=mesh, in_specs=in_specs, out_specs=out_specs, check_vma=False)
```

```python
import functools

import jax
import jax.numpy as jnp
from jax import lax
from jax.experimental import pallas as pl
from jax.experimental.pallas import tpu as pltpu
from jax.sharding import PartitionSpec as P

beta_first = 0.9
beta_second = 0.95
learn_rate = 0.01
decay_rate = 0.1
epsilon = 1e-08

MESH = pl.DeviceIdType.MESH
LANES = 128
SLOT = 8
F32 = jnp.float32
BF16 = jnp.bfloat16


def one_hot(cond):
    return jnp.where(cond, 1.0, 0.0).astype(BF16)


def dot(a, b):
    return jnp.dot(a, b, preferred_element_type=F32)


def iota(shape, axis):
    return lax.broadcasted_iota(jnp.int32, shape, axis)


def ranks(ids_ref):
    n = ids_ref.shape[1]
    lane = jnp.broadcast_to(ids_ref[...].astype(F32), (n, n))
    sub = lane.T
    same = jnp.where(lane == sub, 1.0, 0.0)
    i, j = iota((n, n), 0), iota((n, n), 1)
    within_lane = jnp.sum(jnp.where(i < j, same, 0.0), axis=0, keepdims=True)
    within_sub = jnp.sum(jnp.where(j < i, same, 0.0), axis=1, keepdims=True)
    return lane[0:1].astype(jnp.int32), within_lane.astype(jnp.int32), sub, within_sub


def adam_update(master, first_old, second_old, gradient):
    first_new = beta_first * first_old + (1.0 - beta_first) * gradient
    second_new = beta_second * second_old + (1.0 - beta_second) * gradient * gradient
    master_new = master - learn_rate * (
        first_new / (jnp.sqrt(second_new) + epsilon) + decay_rate * master
    )
    return (master_new, first_new, second_new)


STAGGER = 0


def step_kernel(
    n_e,
    n_p,
    ids_ref,
    owner_ref,
    act_any,
    grad_any,
    gate_up_any,
    down_any,
    master_any,
    first_any,
    second_any,
    ig_ref,
    moved_ref,
    act,
    grad,
    raw,
    gate_up,
    down,
    master,
    first,
    second,
    send,
    slots,
    grads,
    picks,
    mids,
    back,
    msg,
    parts,
    begin,
    ring,
    other,
    csend,
    crecv,
    place_ref,
    msend,
    load_sem,
    keep_sem,
    ssem,
    rsem,
    fssem,
    frsem,
    ring_s,
    ring_r,
    xsem,
    cs_sem,
    cr_sem,
    ms_sem,
    mr_sem,
):
    me, core, dp = lax.axis_index("expert"), lax.axis_index("cuts"), lax.axis_index("dp")
    rows, half = act.shape
    width = 2 * half
    total = n_e * SLOT
    shard = master.shape[1]
    hop = shard // 2
    piece = shard // n_e
    per_half = half // shard
    sibling = {"cuts": 1 - core}
    ahead = ({"dp": (dp + 1) % n_p}, {"dp": (dp + n_p - 1) % n_p})

    def peer(d):
        return (me + d) % n_e

    def block(k):
        return pl.ds(pl.multiple_of(k * SLOT, SLOT), SLOT)

    columns = pl.ds(pl.multiple_of(core * half, half), half)
    loads = [
        pltpu.make_async_copy(src, dst, load_sem.at[i])
        for i, (src, dst) in enumerate(
            (
                (act_any.at[:, columns], act),
                (grad_any.at[:, columns], grad),
                (gate_up_any, raw),
                (down_any, down),
                (master_any, master),
                (first_any, first),
                (second_any, second),
            )
        )
    ]
    for load in loads:
        load.start()

    barrier = pltpu.get_barrier_semaphore()

    @pl.loop(1, n_e)
    def _(d):
        pl.semaphore_signal(
            barrier, inc=1, device_id={"expert": peer(d)}, device_id_type=MESH
        )

    for to in (sibling, *ahead):
        pl.semaphore_signal(barrier, inc=1, device_id=to, device_id_type=MESH)

    ids, within, _, _ = ranks(ids_ref)
    row = iota((total, rows), 0)
    code_in = ids * SLOT + within
    code_grad = jnp.where(within < 3, ids * SLOT + 5 + within, -1)
    pick = jnp.concatenate([one_hot(row == code_in), one_hot(row == code_grad)], axis=1)
    code_rest = jnp.where(within >= 3, ids * SLOT + within - 3, -1000)
    pick_rest = jnp.concatenate([one_hot(row == code_rest + 2 * l) for l in range(4)], axis=1)
    loads[0].wait()
    loads[1].wait()
    send[:, :half] = dot(pick, jnp.concatenate([act[...], grad[...]], axis=0)).astype(BF16)
    for u in range(2):
        tiles = [grad[:, (4 * u + l) * LANES : (4 * u + l + 1) * LANES] for l in range(4)]
        send[:, half + u * LANES : half + (u + 1) * LANES] = dot(
            pick_rest, jnp.concatenate(tiles, axis=0)
        ).astype(BF16)

    pl.semaphore_wait(barrier, n_e + 2)

    def out_copy(d):
        return pltpu.make_async_remote_copy(
            src_ref=send.at[block(peer(d))],
            dst_ref=slots.at[core, block(me)],
            send_sem=ssem.at[d],
            recv_sem=rsem.at[d],
            device_id={"expert": peer(d)},
            device_id_type=MESH,
        )

    def forward(d, from_core):
        at = slots.at[from_core, block((me + n_e - d) % n_e)]
        return pltpu.make_async_remote_copy(
            src_ref=at,
            dst_ref=at,
            send_sem=fssem.at[d],
            recv_sem=frsem.at[d],
            device_id=sibling,
            device_id_type=MESH,
        )

    @pl.loop(1, n_e)
    def _(d):
        out_copy(d).start()

    own = pltpu.make_async_copy(send.at[block(me)], slots.at[core, block(me)], keep_sem.at[0])
    own.start()
    own.wait()
    forward(0, core).start()

    loads[2].wait()
    lines = 256

    @pl.loop(0, width // lines)
    def _(i):
        at = pl.ds(pl.multiple_of(i * lines, lines), lines)
        gate_up[:, at, :] = jnp.swapaxes(raw[at], 0, 1)

    row2 = iota((total, total), 0)
    col2 = iota((total, total), 1)
    place = row2 % SLOT
    for l in range(4):
        picks[l, :, :total] = one_hot((place < 3) & (col2 == row2 + 5))
        picks[l, :, total:] = one_hot(
            ((place == 3) | (place == 4)) & (col2 == row2 - 3 + 2 * l)
        )
    owners = jnp.where(
        iota((n_e, n_e), 0) == me, owner_ref[...].astype(F32), 0.0
    ).astype(BF16)
    spread = one_hot(iota((n_e, shard), 1) // piece == iota((n_e, shard), 0))
    owner_of = jnp.sum(dot(owners, spread), axis=0, keepdims=True).astype(jnp.int32)
    code = owner_of * SLOT + iota((1, shard), 1) % piece
    place_ref[...] = one_hot(iota((total, shard), 0) == code)
    for load in loads[3:]:
        load.wait()

    @pl.loop(1, n_e)
    def _(d):
        out_copy(d).wait_recv()
        forward(d, core).start()

    @pl.loop(0, n_e)
    def _(d):
        forward(d, 1 - core).wait_recv()

    for h in range(2):
        for t in range(half // LANES):
            u, l = t // 4, t % 4
            source = jnp.concatenate(
                [
                    slots[h, :, t * LANES : (t + 1) * LANES],
                    slots[h, :, half + u * LANES : half + (u + 1) * LANES],
                ],
                axis=0,
            )
            grads[:, h * half + t * LANES : h * half + (t + 1) * LANES] = dot(
                picks[l], source
            ).astype(BF16)
    low, high = slots[0, :, :half], slots[1, :, :half]
    gate = dot(low, gate_up[0, :half]) + dot(high, gate_up[0, half:])
    lift = dot(low, gate_up[1, :half]) + dot(high, gate_up[1, half:])
    hidden_grad = dot(grads[...], down[...])
    sigmoid_gate = jax.nn.sigmoid(gate)
    silu_gate = gate * sigmoid_gate
    mids[0] = (hidden_grad * lift * sigmoid_gate * (1.0 + gate * (1.0 - sigmoid_gate))).astype(
        BF16
    )
    mids[1] = (hidden_grad * silu_gate).astype(BF16)
    mids[2] = (silu_gate * lift).astype(BF16)

    def shard_of(t, way):
        return (dp + n_p - 1 - t) % n_p if way == 0 else (dp + 1 + t) % n_p

    def share(g, q, way):
        if g < 2:
            at = pl.ds(pl.multiple_of((q % per_half) * shard, shard), shard)
            lhs = slots[q // per_half, :, at]
        else:
            lhs = grads[:, pl.ds(pl.multiple_of(q * shard, shard), shard)]
        return dot(lhs.T[way * hop : (way + 1) * hop], mids[g])

    def ring_copy(t, g, way, src):
        return pltpu.make_async_remote_copy(
            src_ref=src,
            dst_ref=ring.at[t, g, way],
            send_sem=ring_s.at[t, g, way],
            recv_sem=ring_r.at[t, g, way],
            device_id=ahead[way],
            device_id_type=MESH,
        )

    def ring_start(g):
        for way in range(2):
            begin[g, way] = share(g, shard_of(0, way), way).astype(BF16)
            ring_copy(0, g, way, begin.at[g, way]).start()

    def ring_step(step, active, extra):
        for g in active:
            for way in range(2):
                parts[g, way] = share(g, shard_of(step - g * STAGGER, way), way)
        if extra is not None:
            extra(step)
        for g in active:
            for way in range(2):
                t = step - g * STAGGER
                held = ring.at[t - 1, g, way]
                ring_copy(t - 1, g, way, held).wait_recv()
                held[...] = (held[...].astype(F32) + parts[g, way]).astype(BF16)
                ring_copy(t, g, way, held).start()

    tile = 256
    over_units = (((1,), (1,)), ((), ()))

    def rows_back(step):
        for j in range(2):
            wide = pl.ds(pl.multiple_of((step - 1) * (2 * tile) + j * tile, tile), tile)
            back[:, wide] = (
                lax.dot_general(
                    mids[0], gate_up[0, wide, :], over_units, preferred_element_type=F32
                )
                + lax.dot_general(
                    mids[1], gate_up[1, wide, :], over_units, preferred_element_type=F32
                )
            ).astype(BF16)

    back_steps = width // (2 * tile)

    def pack_back(step):
        m = step - 1 - back_steps
        shift = jnp.concatenate(
            [one_hot((place == 5 + t) & (col2 == row2 - 5 - t + m)) for t in range(3)], axis=1
        )
        for h in range(2):
            rest = jnp.concatenate(
                [back[:, h * half + (5 + t) * LANES : h * half + (6 + t) * LANES] for t in range(3)],
                axis=0,
            )
            base = back[:, pl.ds(pl.multiple_of(h * half + m * LANES, LANES), LANES)]
            msg[h, :, pl.ds(pl.multiple_of(m * LANES, LANES), LANES)] = (
                base.astype(F32) + dot(shift, rest)
            ).astype(BF16)

    swap = pltpu.make_async_remote_copy(
        src_ref=msg.at[1 - core],
        dst_ref=other,
        send_sem=xsem.at[0],
        recv_sem=xsem.at[1],
        device_id=sibling,
        device_id_type=MESH,
    )

    def combine_copy(d):
        return pltpu.make_async_remote_copy(
            src_ref=csend.at[block(peer(d))],
            dst_ref=crecv.at[block(me)],
            send_sem=cs_sem.at[d],
            recv_sem=cr_sem.at[d],
            device_id={"expert": peer(d)},
            device_id_type=MESH,
        )

    keep = pltpu.make_async_copy(csend.at[block(me)], crecv.at[block(me)], keep_sem.at[1])

    def combine(step):
        swap.wait_recv()
        csend[...] = (msg[core].astype(F32) + other[...].astype(F32)).astype(BF16)

        @pl.loop(1, n_e)
        def _(d):
            combine_copy(d).start()

        keep.start()

    def move_copy(g, d):
        return pltpu.make_async_remote_copy(
            src_ref=msend.at[g, peer(d)],
            dst_ref=moved_ref.at[me, :, g],
            send_sem=ms_sem.at[g, d],
            recv_sem=mr_sem.at[g, d],
            device_id={"expert": peer(d)},
            device_id_type=MESH,
        )

    def move_keep(g):
        return pltpu.make_async_copy(
            msend.at[g, me], moved_ref.at[me, :, g], keep_sem.at[2 + g]
        )

    last = n_p - 2

    def finish(g):
        sums = []
        for way in range(2):
            held = ring.at[last, g, way]
            ring_copy(last, g, way, held).wait_recv()
            sums.append(held[...].astype(F32) + parts[g, way])
        gradient = jnp.concatenate(sums, axis=0) * (1.0 / n_p)
        new = adam_update(
            master[g], first[g].astype(F32), second[g].astype(F32), gradient
        )
        for k in range(3):
            placed = dot(place_ref[...], new[k].astype(BF16))
            placed = placed.reshape(n_e, SLOT, placed.shape[1])
            msend[g, :, k] = placed[:, :piece].astype(BF16)

        @pl.loop(1, n_e)
        def _(d):
            move_copy(g, d).start()

        move_keep(g).start()

    def plan(step):
        starts = tuple(g for g in range(3) if step == g * STAGGER)
        active = tuple(g for g in range(3) if 1 <= step - g * STAGGER <= last)
        ends = tuple(g for g in range(3) if step - g * STAGGER == last + 1)
        if 1 <= step <= back_steps:
            extra = rows_back
        elif back_steps < step <= back_steps + 5:
            extra = pack_back
        else:
            extra = None
        return starts, active, ends, extra

    swap_at = back_steps + 6
    step, stop = 0, last + 2 + 2 * STAGGER
    while step < stop:
        starts, active, ends, extra = plan(step)
        if step == swap_at:
            swap.start()
        if step == swap_at + 1:
            extra = combine
        special = starts or ends or step in (swap_at, swap_at + 1)
        until = step + 1
        while not special and until < stop and until not in (swap_at, swap_at + 1):
            if plan(until) != (starts, active, ends, extra):
                break
            until += 1
        if until - step > 1:

            @pl.loop(step, until)
            def _(s, active=active, extra=extra):
                ring_step(s, active, extra)

        else:
            ring_step(step, active, extra)
        for g in starts:
            ring_start(g)
        for g in ends:
            for way in range(2):
                parts[g, way] = share(g, dp, way)
            finish(g)
        step = until

    keep.wait()

    @pl.loop(1, n_e)
    def _(d):
        combine_copy(d).wait_recv()

    _, _, expert, within = ranks(ids_ref)
    expert = jnp.broadcast_to(expert[:, 0:1], (rows, total)).astype(jnp.int32)
    within = jnp.broadcast_to(within, (rows, total)).astype(jnp.int32)
    col = iota((rows, total), 1)
    ig_ref[:, : 5 * LANES] = dot(
        one_hot(col == expert * SLOT + within), crecv[...]
    ).astype(BF16)
    stacked = jnp.concatenate(
        [crecv[:, m * LANES : (m + 1) * LANES] for m in range(5)], axis=0
    )
    for t in range(3):
        pick = jnp.concatenate(
            [one_hot((col == expert * SLOT + 5 + t) & (within == m)) for m in range(5)], axis=1
        )
        ig_ref[:, (5 + t) * LANES : (6 + t) * LANES] = dot(pick, stacked).astype(BF16)

    swap.wait_send()

    @pl.loop(1, n_e)
    def _(d):
        out_copy(d).wait_send()
        combine_copy(d).wait_send()

    @pl.loop(0, n_e)
    def _(d):
        forward(d, core).wait_send()

    @pl.loop(0, n_p - 1)
    def _(t):
        for g in range(3):
            for way in range(2):
                ring_copy(t, g, way, ring.at[t, g, way]).wait_send()

    for g in range(3):
        move_keep(g).wait()

        @pl.loop(1, n_e)
        def _(d, g=g):
            move_copy(g, d).wait_recv()
            move_copy(g, d).wait_send()


def deliver_kernel(ig_in, moved_ref, ig_ref, master_ref, first_ref, second_ref):
    ig_ref[...] = ig_in[...]
    master_ref[...] = moved_ref[:, 0].astype(F32)
    first_ref[...] = moved_ref[:, 1]
    second_ref[...] = moved_ref[:, 2]


VMEM = pl.BlockSpec(memory_space=pltpu.VMEM)
ANY = pl.BlockSpec(memory_space=pl.ANY)


def local(
    activations,
    out_grad,
    expert_ids,
    gate_up_weight,
    down_weight,
    master_weight,
    first_moment,
    second_moment,
    new_owner,
):
    n_e = lax.axis_size("expert")
    n_p = lax.axis_size("dp")
    rows, width = activations.shape
    units = down_weight.shape[2]
    half = width // 2
    total = n_e * SLOT
    shard = width // n_p
    piece = shard // n_e
    line = half + 2 * LANES
    dma = pltpu.SemaphoreType.DMA

    def vmem(*shape, dtype=BF16):
        return pltpu.VMEM(shape, dtype)

    input_grad, moved = pl.pallas_call(
        functools.partial(step_kernel, n_e, n_p),
        name="step",
        out_shape=(
            jax.ShapeDtypeStruct((rows, half), BF16),
            jax.ShapeDtypeStruct((n_e, 3, 3, piece, units), BF16),
        ),
        in_specs=[VMEM] * 2 + [ANY] * 7,
        out_specs=(VMEM, VMEM),
        scratch_shapes=[
            vmem(rows, half),
            vmem(rows, half),
            vmem(width, 2, units),
            vmem(2, width, units),
            vmem(width, units),
            vmem(3, shard, units, dtype=F32),
            vmem(3, shard, units),
            vmem(3, shard, units),
            vmem(total, line),
            vmem(2, total, line),
            vmem(total, width),
            vmem(4, total, 2 * total),
            vmem(3, total, units),
            vmem(total, width),
            vmem(2, total, 5 * LANES),
            vmem(3, 2, shard // 2, units, dtype=F32),
            vmem(3, 2, shard // 2, units),
            vmem(n_p - 1, 3, 2, shard // 2, units),
            vmem(total, 5 * LANES),
            vmem(total, 5 * LANES),
            vmem(total, 5 * LANES),
            vmem(total, shard),
            vmem(3, n_e, 3, piece, units),
            dma((7,)),
            dma((5,)),
            dma((n_e,)),
            dma((n_e,)),
            dma((n_e,)),
            dma((n_e,)),
            dma((n_p - 1, 3, 2)),
            dma((n_p - 1, 3, 2)),
            dma((2,)),
            dma((n_e,)),
            dma((n_e,)),
            dma((3, n_e)),
            dma((3, n_e)),
        ],
        compiler_params=pltpu.CompilerParams(collective_id=0, has_side_effects=True),
    )(
        expert_ids.reshape(1, rows),
        new_owner,
        activations,
        out_grad,
        gate_up_weight[0],
        down_weight[0],
        jnp.moveaxis(master_weight[0], 1, 0),
        jnp.moveaxis(first_moment[0], 1, 0),
        jnp.moveaxis(second_moment[0], 1, 0),
    )
    block = (n_e, 3, piece, units)
    input_grad, *moved = pl.pallas_call(
        deliver_kernel,
        name="deliver",
        out_shape=(
            jax.ShapeDtypeStruct((rows, half), BF16),
            jax.ShapeDtypeStruct(block, F32),
            jax.ShapeDtypeStruct(block, BF16),
            jax.ShapeDtypeStruct(block, BF16),
        ),
        in_specs=[VMEM] * 2,
        out_specs=(VMEM,) * 4,
    )(input_grad, moved)
    return (input_grad, *(jnp.moveaxis(array, 1, 2)[None] for array in moved))


def solution(mesh):
    in_specs = (
        P(("expert", "dp"), None),
        P(("expert", "dp"), None),
        P(("expert", "dp"), None),
        P("expert", None, None, "cuts"),
        P("expert", None, "cuts"),
        P("expert", "dp", None, "cuts"),
        P("expert", "dp", None, "cuts"),
        P("expert", "dp", None, "cuts"),
        P(),
    )
    out_specs = (
        P(("expert", "dp"), "cuts"),
        P("expert", None, "dp", None, "cuts"),
        P("expert", None, "dp", None, "cuts"),
        P("expert", None, "dp", None, "cuts"),
    )
    return jax.shard_map(local, mesh=mesh, in_specs=in_specs, out_specs=out_specs, check_vma=False)
```
